32 devices in a mesh: tm: 4 (over x, core), height: 8 (over z, y).
Axes of the slice: x: 2, y: 2, z: 4, core: 2. Of those that a mesh axis runs over, the one named last changes fastest.
Arguments:
- queries: bfloat16 [16, 64, 4, 1536], P('tm', 'height'), may hold values from -6 to 6
- key_tokens: bfloat16 [16, 64, 4, 1536], P('tm', 'height'), may hold values from -6 to 6
- value_tokens: bfloat16 [16, 64, 4, 1536], P('tm', 'height'), may hold values from -6 to 6
- out_weight: bfloat16 [1536, 3072], P('height'), may hold values from -0.15625 to 0.15625
- out_grad: bfloat16 [16, 64, 4, 3072], P('tm', 'height'), may hold values from -6 to 6
- window_reach: int32 [4, 8, 2], replicated, may hold values from 0 to 2, as said below
- tile_valid: int32 [4, 8], replicated, may hold values 0 or 1
Outputs:
- attn_out: bfloat16 [16, 64, 4, 3072], P('tm', 'height')
- grad_query: bfloat16 [16, 64, 4, 1536], P('tm', 'height')
- grad_key: bfloat16 [16, 64, 4, 1536], P('tm', 'height')
- grad_value: bfloat16 [16, 64, 4, 1536], P('tm', 'height')
- grad_weight: float32 [1536, 3072], P('height', 'tm')
The draws below stay inside these ranges and needn't reach their ends.
Inputs may be any that keep to these rules, and one draw needn't show every extreme that they name: `window_reach`: entry 0 is a tile's reach in frames and entry 1 its reach in rows; some tile reaches 2 in both.
All inputs are finite; a program needn't handle non-finite values.
Results may differ from the reference program's by a relative error of at most 0.014.
Values may be sent and summed in bfloat16 or wider, within the bound.
A program may use at most 128 MiB of HBM per device.

```python
import math
import jax
import jax.numpy as jnp
from jax import lax

D = 3072
HEAD_DIM = 128
HEADS = 12
HD = 1536
TF = 4
TR = 8
COLS = 4
HALO = 2
TOK = 128
TILES_T = 4
TILES_H = 8
FRAMES = 16
ROWS = 64


def drawn_pair(key):
    base_key = jax.random.fold_in(key, 7)
    subkeys = jax.random.split(base_key, 2)
    shape = (FRAMES, ROWS, COLS // 2, 2, HD)
    first = jax.random.truncated_normal(subkeys[0], -6.0, 6.0, shape, jnp.float32)
    second = jax.random.truncated_normal(subkeys[1], -6.0, 6.0, shape, jnp.float32)
    return (first.reshape(FRAMES, ROWS, COLS, HD), second.reshape(FRAMES, ROWS, COLS, HD))


def draw_queries(key, part):
    return drawn_pair(key)[0].astype(jnp.bfloat16)


def draw_key_tokens(key, part):
    return drawn_pair(key)[1].astype(jnp.bfloat16)


def draw_window_reach(key, part):
    subkeys = jax.random.split(jax.random.fold_in(key, 11), 4)
    reach_frame = jax.random.randint(subkeys[0], (TILES_T, TILES_H, 1), 0, HALO + 1, dtype=jnp.int32)
    reach_row = jax.random.randint(subkeys[1], (TILES_T, TILES_H, 1), 0, HALO + 1, dtype=jnp.int32)
    chosen_frame = jax.random.randint(subkeys[2], (), 0, TILES_T, dtype=jnp.int32)
    chosen_row = jax.random.randint(subkeys[3], (), 0, TILES_H, dtype=jnp.int32)
    marked = (jnp.arange(TILES_T, dtype=jnp.int32)[:, None] == chosen_frame) & (jnp.arange(TILES_H, dtype=jnp.int32)[None, :] == chosen_row)
    joined = jnp.concatenate([reach_frame, reach_row], axis=2)
    return jnp.where(marked[:, :, None], jnp.int32(HALO), joined).astype(jnp.int32)


def with_ends(array, rng, low, high):
    extent = array.shape
    spot = [jax.random.randint(jax.random.fold_in(rng, axis), (), 0, extent[axis]) for axis in range(len(extent))]
    array = array.at[tuple(spot)].set(low)
    longest = extent.index(max(extent))
    spot[longest] = (spot[longest] + 1) % extent[longest]
    return array.at[tuple(spot)].set(high)


def spiked(array, key, source, target, blocks, factor):
    owner, partner = [(jnp.arange(array.shape[dim]) // (array.shape[dim] // blocks)).reshape([-1 if axis == dim else 1 for axis in range(array.ndim)]) for dim in (source, target)]
    chosen = jax.random.permutation(key, blocks)[partner]
    strong = (owner == chosen) | (owner == (partner + blocks // 2) % blocks)
    return jnp.where(strong, factor * array, array)


def steps_of(own_key, dims, pieces, least, top_value):
    factor_of = 1.0
    for dim, parts in pieces:
        draws = jax.random.uniform(jax.random.fold_in(jax.random.fold_in(own_key, 6), dim), (parts,), jnp.float32, least / len(pieces), top_value / len(pieces))
        factor_of = factor_of * jnp.repeat(jnp.exp(draws), dims[dim] // parts).reshape((-1,) + (1,) * (len(dims) - 1 - dim))
    return factor_of


def centred(key, dims, width, most, cuts=(), kind=jnp.bfloat16):
    array = width * jax.random.normal(key, dims, jnp.float32)
    if cuts:
        array = array * steps_of(key, dims, cuts, -0.22, 0.18)
    return jnp.clip(array, -most, most).astype(kind)


def bell_draw_with(key, shape, spread, limit, cuts, heavy, kind=jnp.bfloat16):
    values = spread * jax.random.normal(key, shape, jnp.float32)
    if cuts:
        values = values * steps_of(key, shape, cuts, -0.22, 0.18)
    return jnp.clip(spiked(values, jax.random.fold_in(key, 3), *heavy), -limit, limit).astype(kind)


def setup_inputs(seed: int = 0) -> dict:
    seeds = jax.random.split(jax.random.key(seed), 8)
    queries = draw_queries(jax.random.fold_in(seeds[7], 71), 0)
    key_tokens = draw_key_tokens(jax.random.fold_in(seeds[7], 71), 0)
    value_tokens = centred(seeds[2], (FRAMES, ROWS, COLS, HD), 1.0, 6.0, ((0, 4), (1, 8)))
    out_weight = centred(seeds[3], (HD, D), HD ** -0.5, 0.15625, ((0, 8),))
    out_grad = bell_draw_with(seeds[4], (FRAMES, ROWS, COLS, D), 1.0, 6.0, ((0, 4), (1, 8)), (0, 3, 4, 2.0))
    window_reach = draw_window_reach(jax.random.fold_in(seeds[7], 71), 0)
    tile_valid = with_ends((jax.random.randint(seeds[6], (TILES_T, TILES_H), 0, 4) < 3).astype(jnp.int32), jax.random.fold_in(seeds[6], 1), 0, 1)
    return {"queries": queries, "key_tokens": key_tokens, "value_tokens": value_tokens, "out_weight": out_weight, "out_grad": out_grad, "window_reach": window_reach, "tile_valid": tile_valid}


def tile_allowed(window_reach, tile_valid, frame_tile, row_tile):
    ext_frames = TF + 2 * HALO
    ext_rows = TR + 2 * HALO
    frame_pos = jnp.arange(ext_frames, dtype=jnp.int32)
    row_pos = jnp.arange(ext_rows, dtype=jnp.int32)
    global_frame = frame_tile * TF - HALO + frame_pos
    global_row = row_tile * TR - HALO + row_pos
    reach_frame = window_reach[frame_tile, row_tile, 0]
    reach_row = window_reach[frame_tile, row_tile, 1]
    own_frame = (frame_pos >= HALO) & (frame_pos < HALO + TF)
    own_row = (row_pos >= HALO) & (row_pos < HALO + TR)
    near_frame = (frame_pos >= HALO - reach_frame) & (frame_pos < HALO + TF + reach_frame)
    near_frame = near_frame & (global_frame >= 0) & (global_frame < FRAMES)
    near_row = (row_pos >= HALO - reach_row) & (row_pos < HALO + TR + reach_row)
    near_row = near_row & (global_row >= 0) & (global_row < ROWS)
    key_frame_tile = jnp.clip(jnp.floor_divide(global_frame, TF), 0, TILES_T - 1).astype(jnp.int32)
    key_row_tile = jnp.clip(jnp.floor_divide(global_row, TR), 0, TILES_H - 1).astype(jnp.int32)
    valid = tile_valid[key_frame_tile[:, None], key_row_tile[None, :]] == 1
    allowed = own_frame[:, None] & own_row[None, :] | near_frame[:, None] & near_row[None, :] & valid
    return jnp.broadcast_to(allowed[:, :, None], (ext_frames, ext_rows, COLS)).reshape(-1)

def reference(queries, key_tokens, value_tokens, out_weight, out_grad, window_reach, tile_valid):
    ext_frames = TF + 2 * HALO
    ext_rows = TR + 2 * HALO
    ext_count = ext_frames * ext_rows * COLS
    score_scale = 1.0 / math.sqrt(HEAD_DIM)
    d_mixed_all = jnp.dot(out_grad.reshape(-1, D), out_weight.T, preferred_element_type=jnp.float32)
    d_mixed_all = d_mixed_all.astype(jnp.bfloat16).reshape(FRAMES, ROWS, COLS, HD)
    padding = ((HALO, HALO), (HALO, HALO), (0, 0), (0, 0))
    padded_keys = jnp.pad(key_tokens, padding)
    padded_values = jnp.pad(value_tokens, padding)
    zero_grads = jnp.zeros((FRAMES + 2 * HALO, ROWS + 2 * HALO, COLS, HD), jnp.float32)
    zero_weight = jnp.zeros((HD, D), jnp.float32)

    def one_tile(carry, tile_index):
        key_acc, value_acc, weight_acc = carry
        frame_tile = (tile_index // TILES_H).astype(jnp.int32)
        row_tile = (tile_index % TILES_H).astype(jnp.int32)
        start_frame = (frame_tile * TF).astype(jnp.int32)
        start_row = (row_tile * TR).astype(jnp.int32)
        zero_index = jnp.zeros((), jnp.int32)
        corner = (start_frame, start_row, zero_index, zero_index)
        q_tile = lax.dynamic_slice(queries, corner, (TF, TR, COLS, HD)).reshape(TOK, HEADS, HEAD_DIM)
        dm_tile = lax.dynamic_slice(d_mixed_all, corner, (TF, TR, COLS, HD)).reshape(TOK, HEADS, HEAD_DIM)
        grad_tile = lax.dynamic_slice(out_grad, corner, (TF, TR, COLS, D)).reshape(TOK, D)
        k_ext = lax.dynamic_slice(padded_keys, corner, (ext_frames, ext_rows, COLS, HD)).reshape(ext_count, HEADS, HEAD_DIM)
        v_ext = lax.dynamic_slice(padded_values, corner, (ext_frames, ext_rows, COLS, HD)).reshape(ext_count, HEADS, HEAD_DIM)
        allowed = tile_allowed(window_reach, tile_valid, frame_tile, row_tile)
        q32 = q_tile.astype(jnp.float32)
        k32 = k_ext.astype(jnp.float32)
        v32 = v_ext.astype(jnp.float32)
        dm32 = dm_tile.astype(jnp.float32)
        scores = jnp.einsum('qhd,khd->hqk', q32, k32) * score_scale
        scores = jnp.where(allowed[None, None, :], scores, -1e+30)
        row_max = lax.optimization_barrier(jnp.max(scores, axis=-1, keepdims=True))
        expo = jnp.exp(scores - row_max)
        prob = expo / lax.optimization_barrier(jnp.sum(expo, axis=-1, keepdims=True))
        probs = prob.astype(jnp.bfloat16)
        probs32 = probs.astype(jnp.float32)
        mixed = jnp.einsum('hqk,khd->qhd', probs32, v32).astype(jnp.bfloat16)
        d_probs = jnp.einsum('qhd,khd->hqk', dm32, v32)
        inner = lax.optimization_barrier(jnp.sum(prob * d_probs, axis=-1, keepdims=True))
        d_scores = (prob * (d_probs - inner) * score_scale).astype(jnp.bfloat16).astype(jnp.float32)
        d_query = jnp.einsum('hqk,khd->qhd', d_scores, k32).astype(jnp.bfloat16)
        d_key = jnp.einsum('hqk,qhd->khd', d_scores, q32).reshape(ext_frames, ext_rows, COLS, HD)
        d_value = jnp.einsum('hqk,qhd->khd', probs32, dm32).reshape(ext_frames, ext_rows, COLS, HD)
        key_acc = lax.dynamic_update_slice(key_acc, lax.dynamic_slice(key_acc, corner, (ext_frames, ext_rows, COLS, HD)) + d_key, corner)
        value_acc = lax.dynamic_update_slice(value_acc, lax.dynamic_slice(value_acc, corner, (ext_frames, ext_rows, COLS, HD)) + d_value, corner)
        mixed_rows = mixed.reshape(TOK, HD)
        term = jnp.dot(mixed_rows.T, grad_tile, preferred_element_type=jnp.float32).astype(jnp.bfloat16)
        term = lax.optimization_barrier(term).astype(jnp.float32)
        return ((key_acc, value_acc, weight_acc + term), (mixed, d_query))
    tile_ids = jnp.arange(TILES_T * TILES_H, dtype=jnp.int32)
    carry, stacked = lax.scan(one_tile, (zero_grads, zero_grads, zero_weight), tile_ids)
    key_acc, value_acc, grad_weight = carry
    mixed_tiles, dq_tiles = stacked

    def untile(tiles):
        shaped = tiles.reshape(TILES_T, TILES_H, TF, TR, COLS, HD)
        return shaped.transpose(0, 2, 1, 3, 4, 5).reshape(FRAMES, ROWS, COLS, HD)
    mixed_all = untile(mixed_tiles)
    grad_query = untile(dq_tiles)
    attn_out = jnp.dot(mixed_all.reshape(-1, HD), out_weight, preferred_element_type=jnp.float32)
    attn_out = attn_out.astype(jnp.bfloat16).reshape(FRAMES, ROWS, COLS, D)
    grad_key = key_acc[HALO:HALO + FRAMES, HALO:HALO + ROWS].astype(jnp.bfloat16)
    grad_value = value_acc[HALO:HALO + FRAMES, HALO:HALO + ROWS].astype(jnp.bfloat16)
    return (attn_out, grad_query, grad_key, grad_value, grad_weight)
```

```python
import functools
import math

import jax
import jax.numpy as jnp
import numpy as np
from jax import lax
from jax.experimental import pallas as pl
from jax.experimental.pallas import tpu as pltpu
from jax.sharding import PartitionSpec as P

HEAD_DIM = 128
HALO = 2
MESH = pl.DeviceIdType.MESH
F32 = jnp.float32
BF16 = jnp.bfloat16
SIDES = ((-1, 0), (1, 0), (0, -1), (0, 1), (-1, -1), (-1, 1), (1, -1), (1, 1))


def piece_sizes(frames, rows, columns):
    sizes = []
    for df, dr in SIDES:
        sizes.append((HALO if df else frames) * (HALO if dr else rows) * columns)
    return sizes


def key_bias(window_reach, tile_valid, t, h, frames, rows, columns):
    tables = []
    for df, dr in ((0, 0),) + SIDES:
        fs = range(HALO) if df else range(frames)
        rs = range(HALO) if dr else range(rows)
        for f in fs:
            for r in rs:
                fd = 0 if df == 0 else (HALO - f if df < 0 else f + 1)
                rd = 0 if dr == 0 else (HALO - r if dr < 0 else r + 1)
                tables += [(df, dr, fd, rd)] * columns
    table = np.array(tables, np.int32)
    df, dr, fd, rd = (jnp.asarray(table[:, i]) for i in range(4))
    nt, nh = tile_valid.shape
    ti = jnp.arange(nt, dtype=jnp.int32)[:, None]
    hi = jnp.arange(nh, dtype=jnp.int32)[None, :]
    mine = ((ti == t) & (hi == h)).astype(jnp.int32)
    reach = jnp.sum(window_reach * mine[:, :, None], axis=(0, 1))
    hit = (ti[None] == (t + df)[:, None, None]) & (hi[None] == (h + dr)[:, None, None])
    valid = jnp.sum(jnp.where(hit, tile_valid[None], 0), axis=(1, 2)) > 0
    own = (df == 0) & (dr == 0)
    allowed = own | ((fd <= reach[0]) & (rd <= reach[1]) & valid)
    return jnp.where(allowed, 0.0, -1e30).astype(F32)[None, :]


def piece_rows(df, dr, frames, rows, columns):
    fs = range(frames) if df == 0 else (range(frames - HALO, frames) if df < 0 else range(HALO))
    if dr == 0:
        return [(fs[0] * rows * columns, len(fs) * rows * columns)]
    first = (rows - HALO) if dr < 0 else 0
    return [((f * rows + first) * columns, HALO * columns) for f in fs]


def kernel(
    dims,
    q_ref, k_ref, v_ref, bias_ref, w_hbm, og_hbm,
    attn_ref, dq_ref, dk_ref, dv_ref, gw_ref,
    wfull, ogfull, kvsend, kvext, gsend, grecv, prob, dmixed, mixed, mixwin, acc, gwin,
    local_sem, halo_s, halo_r, grad_s, grad_r, mix_s, mix_r,
    wr_s, wr_r, wl_s, wl_r, wc_s, wc_r, or_s, or_r, ol_s, ol_r,
):
    nt, nh, frames, rows, columns = dims
    t, h = lax.axis_index("tm"), lax.axis_index("height")
    tokens, width = q_ref.shape
    model = og_hbm.shape[1]
    share = w_hbm.shape[0]
    heads = width // HEAD_DIM
    half = model // 2
    window = mixwin.shape[1]
    scale = 1.0 / math.sqrt(HEAD_DIM)
    sizes = piece_sizes(frames, rows, columns)
    starts = [sum(sizes[:i]) for i in range(8)]

    def place(df, dr):
        return (lax.rem(t + nt + df, nt), lax.rem(h + nh + dr, nh))

    def remote(src, dst, ssem, rsem, where):
        return pltpu.make_async_remote_copy(
            src_ref=src, dst_ref=dst, send_sem=ssem, recv_sem=rsem,
            device_id=where, device_id_type=MESH,
        )

    def wrow(j, lo=0, size=None):
        return pl.ds(pl.multiple_of(j * share + lo, 16), share if size is None else size)

    def orow(j, lo=0, size=None):
        return pl.ds(pl.multiple_of(j * tokens + lo, 16), tokens if size is None else size)

    own_w = pltpu.make_async_copy(w_hbm, wfull.at[wrow(h), :], local_sem.at[0])
    own_og = pltpu.make_async_copy(og_hbm, ogfull.at[orow(h), :], local_sem.at[1])
    own_w.start()
    own_og.start()

    barrier = pltpu.get_barrier_semaphore()
    greeted = 0
    for i in range(1, nh):
        pl.semaphore_signal(barrier, inc=1, device_id=(t, lax.rem(h + i, nh)), device_id_type=MESH)
        greeted += 1
    for df, dr in SIDES:
        if df:
            pl.semaphore_signal(barrier, inc=1, device_id=place(df, dr), device_id_type=MESH)
            greeted += 1

    for i, ref in enumerate((k_ref, v_ref)):
        x = ref[...]
        kvext[i, 0:tokens, :] = x
        x = x.astype(F32)
        for s, (df, dr) in enumerate(SIDES):
            parts = [x[a : a + n] for a, n in piece_rows(df, dr, frames, rows, columns)]
            y = parts[0] if len(parts) == 1 else jnp.concatenate(parts, axis=0)
            kvsend[i, starts[s] : starts[s] + sizes[s], :] = y.astype(BF16)

    pl.semaphore_wait(barrier, greeted)
    halos = []
    for s, (df, dr) in enumerate(SIDES):
        copy = remote(
            kvsend.at[:, pl.ds(starts[s], sizes[s]), :],
            kvext.at[:, pl.ds(tokens + starts[s], sizes[s]), :],
            halo_s.at[s], halo_r.at[s], place(-df, -dr),
        )
        copy.start()
        halos.append(copy)

    par = lax.rem(h, 2)
    pos = (1 - par) * (h // 2) + par * (nh - 1 - h // 2)

    def at(p):
        p = lax.rem(p + nh, nh)
        far = p // (nh // 2)
        return (1 - far) * (2 * p) + far * (2 * (nh - 1 - p) + 1)

    right, left = (t, at(pos + 1)), (t, at(pos - 1))
    steps = nh // 2
    core = lax.rem(t, 2)
    partner = (t + 1 - 2 * core, h)
    mine = pl.ds(pl.multiple_of(core * half, 128), half)

    def span(step, size, side):
        if step < steps - 1:
            return 0, size
        return (0 if side == 0 else size // 2), size // 2

    def ring_sends(step, buf, rowfn, size, cols, sems):
        out = []
        for side, (target, sign) in enumerate(((right, -1), (left, 1))):
            lo, n = span(step, size, side)
            ref = buf.at[rowfn(at(pos + sign * step), lo, n), cols]
            ssem, rsem = sems[2 * side], sems[2 * side + 1]
            copy = remote(ref, ref, ssem.at[step], rsem.at[step], target)
            copy.start()
            out.append(copy)
        return out

    wsems = (wr_s, wr_r, wl_s, wl_r)
    osems = (or_s, or_r, ol_s, ol_r)
    allcols = pl.ds(0, model)

    def w_sends(step):
        return ring_sends(step, wfull, wrow, share, mine, wsems)

    def og_sends(step):
        return ring_sends(step, ogfull, orow, tokens, allcols, osems)

    def core_sends(step):
        out = []
        for side, sign in enumerate((-1, 1)):
            lo, n = span(step, share, side)
            ref = wfull.at[wrow(at(pos + sign * (step + 1)), lo, n), mine]
            copy = remote(ref, ref, wc_s.at[2 * step + side], wc_r.at[2 * step + side], partner)
            copy.start()
            out.append(copy)
        return out

    own_w.wait()
    own_og.wait()
    w_copies = w_sends(0)
    core_copies = []
    w_live = list(w_copies)

    for copy in halos:
        copy.wait()

    group = 3 if heads % 3 == 0 else 1

    def cols_of(c):
        return pl.ds(pl.multiple_of(c * HEAD_DIM, HEAD_DIM), HEAD_DIM)

    def nt_dot(a, b):
        return lax.dot_general(a, b, (((1,), (1,)), ((), ())), preferred_element_type=F32)

    def tn_dot(a, b):
        return lax.dot_general(a, b, (((0,), (0,)), ((), ())), preferred_element_type=F32)

    def nn_dot(a, b):
        return lax.dot_general(a, b, (((1,), (0,)), ((), ())), preferred_element_type=F32)

    def forward(g, carry):
        for j in range(group):
            c = g * group + j
            cs = cols_of(c)
            scores = nt_dot(q_ref[:, cs], kvext[0, :, cs]) * scale + bias_ref[...]
            e = jnp.exp(scores - jnp.max(scores, axis=-1, keepdims=True))
            p = e / jnp.sum(e, axis=-1, keepdims=True)
            prob[c] = p
            mixed[:, cs] = nn_dot(p.astype(BF16), kvext[1, :, cs]).astype(BF16)
        return carry

    lax.fori_loop(0, heads // group, forward, 0)

    def window_start(j):
        block = (j * share) // 128
        last = (width - window) // 128
        block = jnp.minimum(block, last)
        return pl.multiple_of(block * 128, 128)

    mixwin[orow(h), :] = mixed[:, pl.ds(window_start(h), window)]
    mix_copies = []
    for i in range(1, nh):
        j = lax.rem(h + i, nh)
        copy = remote(
            mixed.at[:, pl.ds(window_start(j), window)], mixwin.at[orow(h), :],
            mix_s.at[i - 1], mix_r.at[i - 1], (t, j),
        )
        copy.start()
        mix_copies.append(copy)

    og_live = []
    for step in range(steps):
        for copy in w_live:
            copy.wait()
        w_live = []
        if step < steps - 1:
            w_live = w_sends(step + 1)
        else:
            og_live = og_sends(0)
        core_copies += core_sends(step)
    for copy in core_copies:
        copy.wait()

    def project(i, carry):
        r = pl.ds(pl.multiple_of(i * 256, 256), 256)
        dmixed[:, r] = nt_dot(ogfull[orow(h), :], wfull[r, :]).astype(BF16)
        return carry

    lax.fori_loop(0, width // 256, project, 0)

    def backward(g, carry):
        for j in range(group):
            c = g * group + j
            cs = cols_of(c)
            p = prob[c]
            dm = dmixed[:, cs]
            dp = nt_dot(dm, kvext[1, :, cs])
            inner = jnp.sum(p * dp, axis=-1, keepdims=True)
            ds = (p * (dp - inner) * scale).astype(BF16)
            dq_ref[:, cs] = nn_dot(ds, kvext[0, :, cs]).astype(BF16)
            dk = tn_dot(ds, q_ref[:, cs])
            dv = tn_dot(p.astype(BF16), dm)
            acc[0, :, cs] = dk[:tokens]
            acc[1, :, cs] = dv[:tokens]
            gsend[0, :, cs] = dk[tokens:].astype(BF16)
            gsend[1, :, cs] = dv[tokens:].astype(BF16)
        return carry

    lax.fori_loop(0, heads // group, backward, 0)

    grads = []
    for s, (df, dr) in enumerate(SIDES):
        rs = pl.ds(starts[s], sizes[s])
        copy = remote(
            gsend.at[:, rs, :], grecv.at[:, rs, :], grad_s.at[s], grad_r.at[s], place(df, dr)
        )
        copy.start()
        grads.append(copy)

    def og_step(step):
        for copy in og_live:
            copy.wait()
        og_live.clear()
        if step < steps:
            og_live.extend(og_sends(step))

    og_step(1)

    def attn(i, carry):
        cs = pl.ds(pl.multiple_of(i * 256, 256), 256)
        attn_ref[:, cs] = nn_dot(mixed[...], wfull[:, cs]).astype(BF16)
        return carry

    lax.fori_loop(0, model // 256, attn, 0)

    for copy in grads:
        copy.wait()
    for i, ref in enumerate((dk_ref, dv_ref)):
        for s, (df, dr) in enumerate(SIDES):
            y = grecv[i, starts[s] : starts[s] + sizes[s], :].astype(F32)
            first = 0
            for a, n in piece_rows(df, dr, frames, rows, columns):
                acc[i, a : a + n, :] += y[first : first + n]
                first += n
        ref[...] = acc[i].astype(BF16)

    for step in range(2, steps + 1):
        og_step(step)
    for copy in mix_copies:
        copy.wait()

    offset = pl.multiple_of(h * share - window_start(h), 16)

    def weight(i, carry):
        cs = pl.ds(pl.multiple_of(i * 512, 512), 512)
        gwin[...] = tn_dot(mixwin[...], ogfull[:, cs])
        gw_ref[:, cs] = gwin[pl.ds(offset, share), :].astype(BF16)
        return carry

    lax.fori_loop(0, model // 512, weight, 0)


def shards(nt, nh, queries, key_tokens, value_tokens, out_weight, out_grad, window_reach, tile_valid):
    frames, rows, columns, width = queries.shape
    model = out_grad.shape[3]
    share = out_weight.shape[0]
    tokens = frames * rows * columns
    heads = width // HEAD_DIM
    halo = sum(piece_sizes(frames, rows, columns))
    ext = tokens + halo
    window = 256
    t, h = lax.axis_index("tm"), lax.axis_index("height")
    bias = key_bias(window_reach, tile_valid, t, h, frames, rows, columns)
    steps = nh // 2
    vmem = pl.BlockSpec(memory_space=pltpu.VMEM)
    hbm = pl.BlockSpec(memory_space=pl.ANY)
    dma = pltpu.SemaphoreType.DMA
    attn, dq, dk, dv, gw = pl.pallas_call(
        functools.partial(kernel, (nt, nh, frames, rows, columns)),
        out_shape=(
            jax.ShapeDtypeStruct((tokens, model), BF16),
            jax.ShapeDtypeStruct((tokens, width), BF16),
            jax.ShapeDtypeStruct((tokens, width), BF16),
            jax.ShapeDtypeStruct((tokens, width), BF16),
            jax.ShapeDtypeStruct((share, model), BF16),
        ),
        in_specs=[vmem, vmem, vmem, vmem, hbm, hbm],
        out_specs=[vmem] * 5,
        scratch_shapes=[
            pltpu.VMEM((width, model), BF16),
            pltpu.VMEM((nh * tokens, model), BF16),
            pltpu.VMEM((2, halo, width), BF16),
            pltpu.VMEM((2, ext, width), BF16),
            pltpu.VMEM((2, halo, width), BF16),
            pltpu.VMEM((2, halo, width), BF16),
            pltpu.VMEM((heads, tokens, ext), F32),
            pltpu.VMEM((tokens, width), BF16),
            pltpu.VMEM((tokens, width), BF16),
            pltpu.VMEM((nh * tokens, window), BF16),
            pltpu.VMEM((2, tokens, width), F32),
            pltpu.VMEM((window, 512), F32),
            dma((2,)), dma((8,)), dma((8,)), dma((8,)), dma((8,)),
            dma((nh - 1,)), dma((nh - 1,)),
            dma((steps,)), dma((steps,)), dma((steps,)), dma((steps,)),
            dma((2 * steps,)), dma((2 * steps,)),
            dma((steps,)), dma((steps,)), dma((steps,)), dma((steps,)),
        ],
        compiler_params=pltpu.CompilerParams(
            collective_id=0, has_side_effects=True, vmem_limit_bytes=56 * 2**20
        ),
    )(
        queries.reshape(tokens, width),
        key_tokens.reshape(tokens, width),
        value_tokens.reshape(tokens, width),
        bias,
        out_weight,
        out_grad.reshape(tokens, model),
    )
    grad_weight = lax.psum_scatter(gw, "tm", scatter_dimension=1, tiled=True).astype(F32)
    tile = (frames, rows, columns)
    return (
        attn.reshape(*tile, model),
        dq.reshape(*tile, width),
        dk.reshape(*tile, width),
        dv.reshape(*tile, width),
        grad_weight,
    )


def solution(mesh):
    tile = P("tm", "height", None, None)
    return jax.shard_map(
        functools.partial(shards, mesh.shape["tm"], mesh.shape["height"]),
        mesh=mesh,
        in_specs=(tile, tile, tile, P("height", None), tile, P(), P()),
        out_specs=(tile, tile, tile, tile, P("height", "tm")),
        check_vma=False,
    )
```

```python
import functools
import math

import jax
import jax.numpy as jnp
import numpy as np
from jax import lax
from jax.experimental import pallas as pl
from jax.experimental.pallas import tpu as pltpu
from jax.sharding import PartitionSpec as P

HEAD_DIM = 128
HALO = 2
MESH = pl.DeviceIdType.MESH
F32 = jnp.float32
BF16 = jnp.bfloat16
SIDES = ((-1, 0), (1, 0), (0, -1), (0, 1), (-1, -1), (-1, 1), (1, -1), (1, 1))


def piece_sizes(frames, rows, columns):
    sizes = []
    for df, dr in SIDES:
        sizes.append((HALO if df else frames) * (HALO if dr else rows) * columns)
    return sizes


def key_table(frames, rows, columns):
    table = []
    for piece, (df, dr) in enumerate(((0, 0),) + SIDES):
        for f in range(HALO) if df else range(frames):
            for r in range(HALO) if dr else range(rows):
                fd = 0 if df == 0 else (HALO - f if df < 0 else f + 1)
                rd = 0 if dr == 0 else (HALO - r if dr < 0 else r + 1)
                table += [(piece, fd, rd)] * columns
    return np.ascontiguousarray(np.array(table, np.int32).T)


def piece_rows(df, dr, frames, rows, columns):
    fs = range(frames) if df == 0 else (range(frames - HALO, frames) if df < 0 else range(HALO))
    if dr == 0:
        return [(fs[0] * rows * columns, len(fs) * rows * columns)]
    first = (rows - HALO) if dr < 0 else 0
    return [((f * rows + first) * columns, HALO * columns) for f in fs]


def kernel(
    dims,
    q_ref, k_ref, v_ref, table_ref, reach_ref, valid_ref, w_hbm, og_hbm,
    attn_ref, dq_ref, dk_ref, dv_ref, gw_ref,
    wfull, ogfull, kvsend, kvext, gsend, grecv, prob, dmixed, mixed, mixwin, acc, gwin, bias_ref, gwsend, gwrecv,
    local_sem, halo_s, halo_r, grad_s, grad_r, mix_s, mix_r,
    wr_s, wr_r, wl_s, wl_r, wc_s, wc_r, wx_s, wx_r, wf_s, wf_r, or_s, or_r, ol_s, ol_r, gw_s, gw_r,
):
    nt, nh, frames, rows, columns = dims
    t, h = lax.axis_index("tm"), lax.axis_index("height")
    tokens, width = q_ref.shape
    model = og_hbm.shape[1]
    share = w_hbm.shape[0]
    heads = width // HEAD_DIM
    quarter = model // 4
    window = mixwin.shape[1]
    scale = 1.0 / math.sqrt(HEAD_DIM)
    sizes = piece_sizes(frames, rows, columns)
    starts = [sum(sizes[:i]) for i in range(8)]

    def place(df, dr):
        return (lax.rem(t + nt + df, nt), lax.rem(h + nh + dr, nh))

    def exists(df, dr):
        a, b = t + df, h + dr
        return (a >= 0) & (a < nt) & (b >= 0) & (b < nh)

    def exchange(copies, sign, action):
        for (df, dr), copy in zip(SIDES, copies):
            if action == "start":
                pl.when(exists(sign * df, sign * dr))(copy.start)
            else:
                pl.when(exists(sign * df, sign * dr))(copy.wait_send)
                pl.when(exists(-sign * df, -sign * dr))(copy.wait_recv)

    def remote(src, dst, ssem, rsem, where):
        return pltpu.make_async_remote_copy(
            src_ref=src, dst_ref=dst, send_sem=ssem, recv_sem=rsem,
            device_id=where, device_id_type=MESH,
        )

    def wrow(j, lo=0, size=None):
        return pl.ds(pl.multiple_of(j * share + lo, 16), share if size is None else size)

    def orow(j, lo=0, size=None):
        return pl.ds(pl.multiple_of(j * tokens + lo, 16), tokens if size is None else size)

    own_w = pltpu.make_async_copy(w_hbm, wfull.at[wrow(h), :], local_sem.at[0])
    own_og = pltpu.make_async_copy(og_hbm, ogfull.at[orow(h), :], local_sem.at[1])
    own_w.start()
    own_og.start()

    barrier = pltpu.get_barrier_semaphore()
    greeted = 0
    for i in range(1, nh):
        pl.semaphore_signal(barrier, inc=1, device_id=(t, lax.rem(h + i, nh)), device_id_type=MESH)
        greeted += 1
    for i in range(1, nt):
        pl.semaphore_signal(barrier, inc=1, device_id=(lax.rem(t + i, nt), h), device_id_type=MESH)
        greeted += 1
    for df, dr in SIDES:
        if df and dr:
            pl.semaphore_signal(barrier, inc=1, device_id=place(df, dr), device_id_type=MESH)
            greeted += 1

    piece = table_ref[0:1, :]
    hit = jnp.ones_like(piece)
    for s, (df, dr) in enumerate(SIDES):
        a, b = place(df, dr)
        here = jnp.where(exists(df, dr), valid_ref[a, b], 0)
        hit = jnp.where(piece == s + 1, here, hit)
    near = (table_ref[1:2, :] <= reach_ref[t, h, 0]) & (table_ref[2:3, :] <= reach_ref[t, h, 1])
    bias_ref[...] = jnp.where((piece == 0) | (near & (hit == 1)), 0.0, -1e30)

    for i, ref in enumerate((k_ref, v_ref)):
        x = ref[...]
        kvext[i, 0:tokens, :] = x
        x = x.astype(F32)
        for s, (df, dr) in enumerate(SIDES):
            parts = [x[a : a + n] for a, n in piece_rows(df, dr, frames, rows, columns)]
            y = parts[0] if len(parts) == 1 else jnp.concatenate(parts, axis=0)
            kvsend[i, starts[s] : starts[s] + sizes[s], :] = y.astype(BF16)

    for s, (df, dr) in enumerate(SIDES):

        @pl.when(jnp.logical_not(exists(df, dr)))
        def _():
            rs = pl.ds(tokens + starts[s], sizes[s])
            kvext[:, rs, :] = jnp.zeros((2, sizes[s], width), BF16)

    par = lax.rem(h, 2)
    pos = (1 - par) * (h // 2) + par * (nh - 1 - h // 2)

    def at(p):
        p = lax.rem(p + nh, nh)
        far = p // (nh // 2)
        return (1 - far) * (2 * p) + far * (2 * (nh - 1 - p) + 1)

    right, left = (t, at(pos + 1)), (t, at(pos - 1))
    steps = nh // 2
    core = lax.rem(t, 2)
    partner = (t + 1 - 2 * core, h)
    pair = lax.rem(t // 2, 2)
    across = (t + 2 - 4 * pair, h)

    def quarter_of(i):
        return pl.ds(pl.multiple_of(i * quarter, 128), quarter)

    mine = quarter_of(2 * pair + core)
    theirs = quarter_of(2 * (1 - pair) + core)

    def span(step, size, side):
        if step < steps - 1:
            return 0, size
        return (0 if side == 0 else size // 2), size // 2

    def ring_sends(step, buf, rowfn, size, cols, sems):
        out = []
        for side, (target, sign) in enumerate(((right, -1), (left, 1))):
            lo, n = span(step, size, side)
            ref = buf.at[rowfn(at(pos + sign * step), lo, n), cols]
            ssem, rsem = sems[2 * side], sems[2 * side + 1]
            copy = remote(ref, ref, ssem.at[step], rsem.at[step], target)
            copy.start()
            out.append(copy)
        return out

    wsems = (wr_s, wr_r, wl_s, wl_r)
    osems = (or_s, or_r, ol_s, ol_r)
    allcols = pl.ds(0, model)

    def w_sends(step):
        return ring_sends(step, wfull, wrow, share, mine, wsems)

    def og_sends(step):
        return ring_sends(step, ogfull, orow, tokens, allcols, osems)

    def share_sends(step):
        out = []
        for side, sign in enumerate((-1, 1)):
            lo, n = span(step, share, side)
            ref = wfull.at[wrow(at(pos + sign * (step + 1)), lo, n), mine]
            i = 2 * step + side
            out.append(remote(ref, ref, wx_s.at[i], wx_r.at[i], across))
            out.append(remote(ref, ref, wc_s.at[i], wc_r.at[i], partner))
        for copy in out:
            copy.start()
        return out

    def pass_on(step):
        out = []
        for side, sign in enumerate((-1, 1)):
            lo, n = span(step, share, side)
            ref = wfull.at[wrow(at(pos + sign * (step + 1)), lo, n), theirs]
            i = 2 * step + side
            copy = remote(ref, ref, wf_s.at[i], wf_r.at[i], partner)
            copy.start()
            out.append(copy)
        return out

    own_w.wait()
    own_og.wait()
    pl.semaphore_wait(barrier, greeted)
    halos = []
    for s, (df, dr) in enumerate(SIDES):
        copy = remote(
            kvsend.at[:, pl.ds(starts[s], sizes[s]), :],
            kvext.at[:, pl.ds(tokens + starts[s], sizes[s]), :],
            halo_s.at[s], halo_r.at[s], place(-df, -dr),
        )
        halos.append(copy)
    exchange(halos, -1, "start")
    live = w_sends(0)
    shared = []
    for step in range(steps):
        for copy in live:
            copy.wait()
        live = w_sends(step + 1) if step < steps - 1 else og_sends(0)
        shared.append(share_sends(step))
    exchange(halos, -1, "wait")

    group = 3 if heads % 3 == 0 else 1

    def cols_of(c):
        return pl.ds(pl.multiple_of(c * HEAD_DIM, HEAD_DIM), HEAD_DIM)

    def nt_dot(a, b):
        return lax.dot_general(a, b, (((1,), (1,)), ((), ())), preferred_element_type=F32)

    def tn_dot(a, b):
        return lax.dot_general(a, b, (((0,), (0,)), ((), ())), preferred_element_type=F32)

    def nn_dot(a, b):
        return lax.dot_general(a, b, (((1,), (0,)), ((), ())), preferred_element_type=F32)

    def forward(g, carry):
        for j in range(group):
            c = g * group + j
            cs = cols_of(c)
            scores = nt_dot(q_ref[:, cs], kvext[0, :, cs]) * scale + bias_ref[...]
            e = jnp.exp(scores - jnp.max(scores, axis=-1, keepdims=True))
            p = e / jnp.sum(e, axis=-1, keepdims=True)
            prob[c] = p
            mixed[:, cs] = nn_dot(p.astype(BF16), kvext[1, :, cs]).astype(BF16)
        return carry

    lax.fori_loop(0, heads // group, forward, 0)

    def window_start(j):
        block = (j * share) // 128
        last = (width - window) // 128
        block = jnp.minimum(block, last)
        return pl.multiple_of(block * 128, 128)

    mixwin[orow(h), :] = mixed[:, pl.ds(window_start(h), window)]
    mix_copies = []
    for i in range(1, nh):
        j = lax.rem(h + i, nh)
        copy = remote(
            mixed.at[:, pl.ds(window_start(j), window)], mixwin.at[orow(h), :],
            mix_s.at[i - 1], mix_r.at[i - 1], (t, j),
        )
        copy.start()
        mix_copies.append(copy)

    def og_step(step):
        for copy in live:
            copy.wait()
        live.clear()
        if step < steps:
            live.extend(og_sends(step))

    passed = []
    for step in range(steps):
        for copy in shared[step]:
            copy.wait()
        passed += pass_on(step)
        if step == steps // 2:
            og_step(1)
    for copy in passed:
        copy.wait()

    def project(i, carry):
        r = pl.ds(pl.multiple_of(i * 256, 256), 256)
        dmixed[:, r] = nt_dot(ogfull[orow(h), :], wfull[r, :]).astype(BF16)
        return carry

    lax.fori_loop(0, width // 256, project, 0)

    og_step(2)

    def backward(g, carry):
        for j in range(group):
            c = g * group + j
            cs = cols_of(c)
            p = prob[c]
            dm = dmixed[:, cs]
            dp = nt_dot(dm, kvext[1, :, cs])
            inner = jnp.sum(p * dp, axis=-1, keepdims=True)
            ds = (p * (dp - inner) * scale).astype(BF16)
            dq_ref[:, cs] = nn_dot(ds, kvext[0, :, cs]).astype(BF16)
            dk = tn_dot(ds, q_ref[:, cs])
            dv = tn_dot(p.astype(BF16), dm)
            acc[0, :, cs] = dk[:tokens]
            acc[1, :, cs] = dv[:tokens]
            gsend[0, :, cs] = dk[tokens:].astype(BF16)
            gsend[1, :, cs] = dv[tokens:].astype(BF16)
        return carry

    lax.fori_loop(0, heads // group, backward, 0)

    grads = []
    for s, (df, dr) in enumerate(SIDES):
        rs = pl.ds(starts[s], sizes[s])
        copy = remote(
            gsend.at[:, rs, :], grecv.at[:, rs, :], grad_s.at[s], grad_r.at[s], place(df, dr)
        )
        grads.append(copy)
    exchange(grads, 1, "start")
    og_step(3)

    def attn(i, carry):
        cs = pl.ds(pl.multiple_of(i * 256, 256), 256)
        attn_ref[:, cs] = nn_dot(mixed[...], wfull[:, cs]).astype(BF16)
        return carry

    lax.fori_loop(0, model // 256, attn, 0)

    exchange(grads, 1, "wait")
    for i, ref in enumerate((dk_ref, dv_ref)):
        for s, (df, dr) in enumerate(SIDES):

            @pl.when(exists(-df, -dr))
            def _():
                y = grecv[i, starts[s] : starts[s] + sizes[s], :].astype(F32)
                first = 0
                for a, n in piece_rows(df, dr, frames, rows, columns):
                    acc[i, a : a + n, :] += y[first : first + n]
                    first += n

        ref[...] = acc[i].astype(BF16)

    for step in range(4, steps + 1):
        og_step(step)
    for copy in mix_copies:
        copy.wait()

    offset = pl.multiple_of(h * share - window_start(h), 16)

    block = gwin.shape[1]

    def weight(i):
        cs = pl.ds(pl.multiple_of(i * block, 128), block)
        gwin[...] = tn_dot(mixwin[...], ogfull[:, cs])
        return gwin[pl.ds(offset, share), :]

    if gw_ref.shape[1] == model:
        for i in range(model // block):
            gw_ref[:, i * block : (i + 1) * block] = weight(i).astype(BF16)
        return
    terms = []
    for i in range(1, nt):
        j = lax.rem(t + i, nt)
        gwsend[i - 1] = weight(j).astype(BF16)
        copy = remote(gwsend.at[i - 1], gwrecv.at[i - 1], gw_s.at[i - 1], gw_r.at[i - 1], (j, h))
        copy.start()
        terms.append(copy)
    gw_ref[...] = weight(t)
    for copy in terms:
        copy.wait()
    gw_ref[...] += sum(gwrecv[i].astype(F32) for i in range(nt - 1))


def shards(nt, nh, queries, key_tokens, value_tokens, out_weight, out_grad, window_reach, tile_valid):
    frames, rows, columns, width = queries.shape
    model = out_grad.shape[3]
    share = out_weight.shape[0]
    tokens = frames * rows * columns
    heads = width // HEAD_DIM
    halo = sum(piece_sizes(frames, rows, columns))
    ext = tokens + halo
    window = 256
    table = key_table(frames, rows, columns)
    narrow = (model // nt) % 128 == 0
    block = model // nt if narrow else 512
    slots = nt - 1 if narrow else 1
    steps = nh // 2
    vmem = pl.BlockSpec(memory_space=pltpu.VMEM)
    smem = pl.BlockSpec(memory_space=pltpu.SMEM)
    hbm = pl.BlockSpec(memory_space=pl.ANY)
    dma = pltpu.SemaphoreType.DMA
    attn, dq, dk, dv, gw = pl.pallas_call(
        functools.partial(kernel, (nt, nh, frames, rows, columns)),
        out_shape=(
            jax.ShapeDtypeStruct((tokens, model), BF16),
            jax.ShapeDtypeStruct((tokens, width), BF16),
            jax.ShapeDtypeStruct((tokens, width), BF16),
            jax.ShapeDtypeStruct((tokens, width), BF16),
            jax.ShapeDtypeStruct((share, block), F32)
            if narrow
            else jax.ShapeDtypeStruct((share, model), BF16),
        ),
        in_specs=[vmem, vmem, vmem, vmem, smem, smem, hbm, hbm],
        out_specs=[vmem] * 5,
        scratch_shapes=[
            pltpu.VMEM((width, model), BF16),
            pltpu.VMEM((nh * tokens, model), BF16),
            pltpu.VMEM((2, halo, width), BF16),
            pltpu.VMEM((2, ext, width), BF16),
            pltpu.VMEM((2, halo, width), BF16),
            pltpu.VMEM((2, halo, width), BF16),
            pltpu.VMEM((heads, tokens, ext), F32),
            pltpu.VMEM((tokens, width), BF16),
            pltpu.VMEM((tokens, width), BF16),
            pltpu.VMEM((nh * tokens, window), BF16),
            pltpu.VMEM((2, tokens, width), F32),
            pltpu.VMEM((window, block), F32),
            pltpu.VMEM((1, ext), F32),
            pltpu.VMEM((slots, share, block), BF16),
            pltpu.VMEM((slots, share, block), BF16),
            dma((2,)), dma((8,)), dma((8,)), dma((8,)), dma((8,)),
            dma((nh - 1,)), dma((nh - 1,)),
            dma((steps,)), dma((steps,)), dma((steps,)), dma((steps,)),
            dma((2 * steps,)), dma((2 * steps,)), dma((2 * steps,)), dma((2 * steps,)),
            dma((2 * steps,)), dma((2 * steps,)),
            dma((steps,)), dma((steps,)), dma((steps,)), dma((steps,)),
            dma((nt - 1,)), dma((nt - 1,)),
        ],
        compiler_params=pltpu.CompilerParams(
            collective_id=0, has_side_effects=True, vmem_limit_bytes=56 * 2**20
        ),
    )(
        queries.reshape(tokens, width),
        key_tokens.reshape(tokens, width),
        value_tokens.reshape(tokens, width),
        table,
        window_reach,
        tile_valid,
        out_weight,
        out_grad.reshape(tokens, model),
    )
    if not narrow:
        gw = lax.psum_scatter(gw, "tm", scatter_dimension=1, tiled=True).astype(F32)
    tile = (frames, rows, columns)
    return (
        attn.reshape(*tile, model),
        dq.reshape(*tile, width),
        dk.reshape(*tile, width),
        dv.reshape(*tile, width),
        gw,
    )


def solution(mesh):
    tile = P("tm", "height", None, None)
    return jax.shard_map(
        functools.partial(shards, mesh.shape["tm"], mesh.shape["height"]),
        mesh=mesh,
        in_specs=(tile, tile, tile, P("height", None), tile, P(), P()),
        out_specs=(tile, tile, tile, tile, P("height", "tm")),
        check_vma=False,
    )
```

```python
import functools
import math

import jax
import jax.numpy as jnp
import numpy as np
from jax import lax
from jax.experimental import pallas as pl
from jax.experimental.pallas import tpu as pltpu
from jax.sharding import PartitionSpec as P

HEAD_DIM = 128
HALO = 2
MESH = pl.DeviceIdType.MESH
F32 = jnp.float32
BF16 = jnp.bfloat16
SIDES = ((-1, 0), (1, 0), (0, -1), (0, 1), (-1, -1), (-1, 1), (1, -1), (1, 1))


def piece_sizes(frames, rows, columns):
    sizes = []
    for df, dr in SIDES:
        sizes.append((HALO if df else frames) * (HALO if dr else rows) * columns)
    return sizes


def key_table(frames, rows, columns):
    table = []
    for piece, (df, dr) in enumerate(((0, 0),) + SIDES):
        for f in range(HALO) if df else range(frames):
            for r in range(HALO) if dr else range(rows):
                fd = 0 if df == 0 else (HALO - f if df < 0 else f + 1)
                rd = 0 if dr == 0 else (HALO - r if dr < 0 else r + 1)
                table += [(piece, fd, rd)] * columns
    return np.ascontiguousarray(np.array(table, np.int32).T)


def piece_rows(df, dr, frames, rows, columns):
    fs = range(frames) if df == 0 else (range(frames - HALO, frames) if df < 0 else range(HALO))
    if dr == 0:
        return [(fs[0] * rows * columns, len(fs) * rows * columns)]
    first = (rows - HALO) if dr < 0 else 0
    return [((f * rows + first) * columns, HALO * columns) for f in fs]


def kernel(
    dims,
    q_ref, k_ref, v_ref, table_ref, reach_ref, valid_ref, w_hbm, og_hbm,
    attn_ref, dq_ref, dk_ref, dv_ref, gw_ref,
    wfull, ogown, ogcols, kvsend, kvext, gsend, grecv, prob, dmixed, mixed, mixall, acc, gpart, bias_ref, gwsend, gwrecv,
    local_sem, halo_s, halo_r, grad_s, grad_r, mix_s, mix_r,
    wr_s, wr_r, wl_s, wl_r, wc_s, wc_r, wx_s, wx_r, wf_s, wf_r, og_s, og_r, gw_s, gw_r,
):
    nt, nh, frames, rows, columns = dims
    t, h = lax.axis_index("tm"), lax.axis_index("height")
    tokens, width = q_ref.shape
    model = og_hbm.shape[1]
    share = w_hbm.shape[0]
    heads = width // HEAD_DIM
    quarter = model // 4
    window = gpart.shape[1]
    span_cols = model // nt
    scale = 1.0 / math.sqrt(HEAD_DIM)
    sizes = piece_sizes(frames, rows, columns)
    starts = [sum(sizes[:i]) for i in range(8)]

    def place(df, dr):
        return (lax.rem(t + nt + df, nt), lax.rem(h + nh + dr, nh))

    def exists(df, dr):
        a, b = t + df, h + dr
        return (a >= 0) & (a < nt) & (b >= 0) & (b < nh)

    def exchange(copies, sign, action):
        for (df, dr), copy in zip(SIDES, copies):
            if action == "start":
                pl.when(exists(sign * df, sign * dr))(copy.start)
            else:
                pl.when(exists(sign * df, sign * dr))(copy.wait_send)
                pl.when(exists(-sign * df, -sign * dr))(copy.wait_recv)

    def remote(src, dst, ssem, rsem, where):
        return pltpu.make_async_remote_copy(
            src_ref=src, dst_ref=dst, send_sem=ssem, recv_sem=rsem,
            device_id=where, device_id_type=MESH,
        )

    def wrow(j, lo=0, size=None):
        return pl.ds(pl.multiple_of(j * share + lo, 16), share if size is None else size)

    def orow(j, lo=0, size=None):
        return pl.ds(pl.multiple_of(j * tokens + lo, 16), tokens if size is None else size)

    own_w = pltpu.make_async_copy(w_hbm, wfull.at[wrow(h), :], local_sem.at[0])
    own_og = pltpu.make_async_copy(og_hbm, ogown, local_sem.at[1])
    own_w.start()
    own_og.start()

    barrier = pltpu.get_barrier_semaphore()
    greeted = 0
    for i in range(1, nh):
        pl.semaphore_signal(barrier, inc=1, device_id=(t, lax.rem(h + i, nh)), device_id_type=MESH)
        greeted += 1
    for i in range(1, nt):
        pl.semaphore_signal(barrier, inc=1, device_id=(lax.rem(t + i, nt), h), device_id_type=MESH)
        greeted += 1
    for df, dr in SIDES:
        if df and dr:
            pl.semaphore_signal(barrier, inc=1, device_id=place(df, dr), device_id_type=MESH)
            greeted += 1

    piece = table_ref[0:1, :]
    hit = jnp.ones_like(piece)
    for s, (df, dr) in enumerate(SIDES):
        a, b = place(df, dr)
        here = jnp.where(exists(df, dr), valid_ref[a, b], 0)
        hit = jnp.where(piece == s + 1, here, hit)
    near = (table_ref[1:2, :] <= reach_ref[t, h, 0]) & (table_ref[2:3, :] <= reach_ref[t, h, 1])
    bias_ref[...] = jnp.where((piece == 0) | (near & (hit == 1)), 0.0, -1e30)

    for i, ref in enumerate((k_ref, v_ref)):
        x = ref[...]
        kvext[i, 0:tokens, :] = x
        x = x.astype(F32)
        for s, (df, dr) in enumerate(SIDES):
            parts = [x[a : a + n] for a, n in piece_rows(df, dr, frames, rows, columns)]
            y = parts[0] if len(parts) == 1 else jnp.concatenate(parts, axis=0)
            kvsend[i, starts[s] : starts[s] + sizes[s], :] = y.astype(BF16)

    for s, (df, dr) in enumerate(SIDES):

        @pl.when(jnp.logical_not(exists(df, dr)))
        def _():
            rs = pl.ds(tokens + starts[s], sizes[s])
            kvext[:, rs, :] = jnp.zeros((2, sizes[s], width), BF16)

    par = lax.rem(h, 2)
    pos = (1 - par) * (h // 2) + par * (nh - 1 - h // 2)

    def at(p):
        p = lax.rem(p + nh, nh)
        far = p // (nh // 2)
        return (1 - far) * (2 * p) + far * (2 * (nh - 1 - p) + 1)

    right, left = (t, at(pos + 1)), (t, at(pos - 1))
    steps = nh // 2
    core = lax.rem(t, 2)
    partner = (t + 1 - 2 * core, h)
    pair = lax.rem(t // 2, 2)
    across = (t + 2 - 4 * pair, h)

    def quarter_of(i):
        return pl.ds(pl.multiple_of(i * quarter, 128), quarter)

    mine = quarter_of(2 * pair + core)
    theirs = quarter_of(2 * (1 - pair) + core)

    def span(step, size, side):
        if step < steps - 1:
            return 0, size
        return (0 if side == 0 else size // 2), size // 2

    def ring_sends(step, buf, rowfn, size, cols, sems):
        out = []
        for side, (target, sign) in enumerate(((right, -1), (left, 1))):
            lo, n = span(step, size, side)
            ref = buf.at[rowfn(at(pos + sign * step), lo, n), cols]
            ssem, rsem = sems[2 * side], sems[2 * side + 1]
            copy = remote(ref, ref, ssem.at[step], rsem.at[step], target)
            copy.start()
            out.append(copy)
        return out

    wsems = (wr_s, wr_r, wl_s, wl_r)
    def w_sends(step):
        return ring_sends(step, wfull, wrow, share, mine, wsems)

    def gw_sends(step):
        out = []
        for side, (target, sign) in enumerate(((right, 1), (left, -1))):
            base = at(pos + sign * (steps - step)) * share
            cut = share // 2
            for part in range(2):
                if step == 0 and part != side:
                    continue
                rs = slice(part * cut, (part + 1) * cut)
                total = gpart[pl.ds(pl.multiple_of(base + part * cut, 16), cut), :]
                if step > 1 or (step == 1 and part == side):
                    total += gwrecv[side, step - 1, rs, :].astype(F32)
                gwsend[side, step, rs, :] = total.astype(BF16)
            rs = pl.ds(side * cut, cut) if step == 0 else pl.ds(0, share)
            i = side * steps + step
            copy = remote(
                gwsend.at[side, step, rs, :], gwrecv.at[side, step, rs, :],
                gw_s.at[i], gw_r.at[i], target,
            )
            copy.start()
            out.append(copy)
        return out

    def cols_start(j):
        block = jnp.minimum((j * span_cols) // 128, (model - window) // 128)
        return pl.multiple_of(block * 128, 128)

    def share_sends(step):
        out = []
        for side, sign in enumerate((-1, 1)):
            lo, n = span(step, share, side)
            ref = wfull.at[wrow(at(pos + sign * (step + 1)), lo, n), mine]
            i = 2 * step + side
            out.append(remote(ref, ref, wx_s.at[i], wx_r.at[i], across))
            out.append(remote(ref, ref, wc_s.at[i], wc_r.at[i], partner))
        for copy in out:
            copy.start()
        return out

    def pass_on(step):
        out = []
        for side, sign in enumerate((-1, 1)):
            lo, n = span(step, share, side)
            ref = wfull.at[wrow(at(pos + sign * (step + 1)), lo, n), theirs]
            i = 2 * step + side
            copy = remote(ref, ref, wf_s.at[i], wf_r.at[i], partner)
            copy.start()
            out.append(copy)
        return out

    own_w.wait()
    own_og.wait()
    pl.semaphore_wait(barrier, greeted)
    halos = []
    for s, (df, dr) in enumerate(SIDES):
        copy = remote(
            kvsend.at[:, pl.ds(starts[s], sizes[s]), :],
            kvext.at[:, pl.ds(tokens + starts[s], sizes[s]), :],
            halo_s.at[s], halo_r.at[s], place(-df, -dr),
        )
        halos.append(copy)
    exchange(halos, -1, "start")
    live = w_sends(0)
    ogcols[orow(t), :] = ogown[:, pl.ds(cols_start(t), window)]
    gathers = []
    for i in range(1, nt):
        j = lax.rem(t + i, nt)
        copy = remote(
            ogown.at[:, pl.ds(cols_start(j), window)], ogcols.at[orow(t), :],
            og_s.at[i - 1], og_r.at[i - 1], (j, h),
        )
        copy.start()
        gathers.append(copy)
    shared = []
    for step in range(steps):
        for copy in live:
            copy.wait()
        live = w_sends(step + 1) if step < steps - 1 else []
        shared.append(share_sends(step))
    exchange(halos, -1, "wait")

    group = 3 if heads % 3 == 0 else 1

    def cols_of(c):
        return pl.ds(pl.multiple_of(c * HEAD_DIM, HEAD_DIM), HEAD_DIM)

    def nt_dot(a, b):
        return lax.dot_general(a, b, (((1,), (1,)), ((), ())), preferred_element_type=F32)

    def tn_dot(a, b):
        return lax.dot_general(a, b, (((0,), (0,)), ((), ())), preferred_element_type=F32)

    def nn_dot(a, b):
        return lax.dot_general(a, b, (((1,), (0,)), ((), ())), preferred_element_type=F32)

    def forward(g, carry):
        for j in range(group):
            c = g * group + j
            cs = cols_of(c)
            scores = nt_dot(q_ref[:, cs], kvext[0, :, cs]) * scale + bias_ref[...]
            e = jnp.exp(scores - jnp.max(scores, axis=-1, keepdims=True))
            p = e / jnp.sum(e, axis=-1, keepdims=True)
            prob[c] = p
            mixed[:, cs] = nn_dot(p.astype(BF16), kvext[1, :, cs]).astype(BF16)
        return carry

    lax.fori_loop(0, heads // group, forward, 0)

    mixall[orow(t), :] = mixed[...]
    for i in range(1, nt):
        copy = remote(
            mixed, mixall.at[orow(t), :], mix_s.at[i - 1], mix_r.at[i - 1],
            (lax.rem(t + i, nt), h),
        )
        copy.start()
        gathers.append(copy)

    def gw_step(step):
        for copy in live:
            copy.wait()
        live.clear()
        if step < steps:
            live.extend(gw_sends(step))

    passed = []
    for step in range(steps):
        for copy in shared[step]:
            copy.wait()
        passed += pass_on(step)

    for copy in gathers:
        copy.wait()

    def weight(i, carry):
        cs = pl.ds(pl.multiple_of(i * 256, 256), 256)
        gpart[cs, :] = tn_dot(mixall[:, cs], ogcols[...])
        return carry

    lax.fori_loop(0, width // 256, weight, 0)
    gw_step(0)
    for copy in passed:
        copy.wait()

    def project(i, carry):
        r = pl.ds(pl.multiple_of(i * 256, 256), 256)
        dmixed[:, r] = nt_dot(ogown[...], wfull[r, :]).astype(BF16)
        return carry

    lax.fori_loop(0, width // 256, project, 0)

    gw_step(1)

    def backward(g, carry):
        for j in range(group):
            c = g * group + j
            cs = cols_of(c)
            p = prob[c]
            dm = dmixed[:, cs]
            dp = nt_dot(dm, kvext[1, :, cs])
            inner = jnp.sum(p * dp, axis=-1, keepdims=True)
            ds = (p * (dp - inner) * scale).astype(BF16)
            dq_ref[:, cs] = nn_dot(ds, kvext[0, :, cs]).astype(BF16)
            dk = tn_dot(ds, q_ref[:, cs])
            dv = tn_dot(p.astype(BF16), dm)
            acc[0, :, cs] = dk[:tokens]
            acc[1, :, cs] = dv[:tokens]
            gsend[0, :, cs] = dk[tokens:].astype(BF16)
            gsend[1, :, cs] = dv[tokens:].astype(BF16)
        return carry

    lax.fori_loop(0, heads // group, backward, 0)

    grads = []
    for s, (df, dr) in enumerate(SIDES):
        rs = pl.ds(starts[s], sizes[s])
        copy = remote(
            gsend.at[:, rs, :], grecv.at[:, rs, :], grad_s.at[s], grad_r.at[s], place(df, dr)
        )
        grads.append(copy)
    exchange(grads, 1, "start")
    gw_step(2)

    def attn(i, carry):
        cs = pl.ds(pl.multiple_of(i * 256, 256), 256)
        attn_ref[:, cs] = nn_dot(mixed[...], wfull[:, cs]).astype(BF16)
        return carry

    lax.fori_loop(0, model // 256, attn, 0)
    gw_step(3)

    exchange(grads, 1, "wait")
    for i, ref in enumerate((dk_ref, dv_ref)):
        for s, (df, dr) in enumerate(SIDES):

            @pl.when(exists(-df, -dr))
            def _():
                y = grecv[i, starts[s] : starts[s] + sizes[s], :].astype(F32)
                first = 0
                for a, n in piece_rows(df, dr, frames, rows, columns):
                    acc[i, a : a + n, :] += y[first : first + n]
                    first += n

        ref[...] = acc[i].astype(BF16)

    for step in range(4, steps + 1):
        gw_step(step)
    gw_ref[...] = (
        gpart[wrow(h), :]
        + gwrecv[0, steps - 1].astype(F32)
        + gwrecv[1, steps - 1].astype(F32)
    )


def shards(nt, nh, queries, key_tokens, value_tokens, out_weight, out_grad, window_reach, tile_valid):
    frames, rows, columns, width = queries.shape
    model = out_grad.shape[3]
    share = out_weight.shape[0]
    tokens = frames * rows * columns
    heads = width // HEAD_DIM
    halo = sum(piece_sizes(frames, rows, columns))
    ext = tokens + halo
    table = key_table(frames, rows, columns)
    narrow = (model // nt) % 128 == 0
    block = model // nt if narrow else 256
    steps = nh // 2
    vmem = pl.BlockSpec(memory_space=pltpu.VMEM)
    smem = pl.BlockSpec(memory_space=pltpu.SMEM)
    hbm = pl.BlockSpec(memory_space=pl.ANY)
    dma = pltpu.SemaphoreType.DMA
    attn, dq, dk, dv, gw = pl.pallas_call(
        functools.partial(kernel, (nt, nh, frames, rows, columns)),
        out_shape=(
            jax.ShapeDtypeStruct((tokens, model), BF16),
            jax.ShapeDtypeStruct((tokens, width), BF16),
            jax.ShapeDtypeStruct((tokens, width), BF16),
            jax.ShapeDtypeStruct((tokens, width), BF16),
            jax.ShapeDtypeStruct((share, block), F32),
        ),
        in_specs=[vmem, vmem, vmem, vmem, smem, smem, hbm, hbm],
        out_specs=[vmem] * 5,
        scratch_shapes=[
            pltpu.VMEM((width, model), BF16),
            pltpu.VMEM((tokens, model), BF16),
            pltpu.VMEM((nt * tokens, block), BF16),
            pltpu.VMEM((2, halo, width), BF16),
            pltpu.VMEM((2, ext, width), BF16),
            pltpu.VMEM((2, halo, width), BF16),
            pltpu.VMEM((2, halo, width), BF16),
            pltpu.VMEM((heads, tokens, ext), F32),
            pltpu.VMEM((tokens, width), BF16),
            pltpu.VMEM((tokens, width), BF16),
            pltpu.VMEM((nt * tokens, width), BF16),
            pltpu.VMEM((2, tokens, width), F32),
            pltpu.VMEM((width, block), F32),
            pltpu.VMEM((1, ext), F32),
            pltpu.VMEM((2, steps, share, block), BF16),
            pltpu.VMEM((2, steps, share, block), BF16),
            dma((2,)), dma((8,)), dma((8,)), dma((8,)), dma((8,)),
            dma((nt - 1,)), dma((nt - 1,)),
            dma((steps,)), dma((steps,)), dma((steps,)), dma((steps,)),
            dma((2 * steps,)), dma((2 * steps,)), dma((2 * steps,)), dma((2 * steps,)),
            dma((2 * steps,)), dma((2 * steps,)),
            dma((nt - 1,)), dma((nt - 1,)), dma((2 * steps,)), dma((2 * steps,)),
        ],
        compiler_params=pltpu.CompilerParams(
            collective_id=0, has_side_effects=True, vmem_limit_bytes=56 * 2**20
        ),
    )(
        queries.reshape(tokens, width),
        key_tokens.reshape(tokens, width),
        value_tokens.reshape(tokens, width),
        table,
        window_reach,
        tile_valid,
        out_weight,
        out_grad.reshape(tokens, model),
    )
    if not narrow:
        size = model // nt
        at = lax.axis_index("tm") * size
        first = jnp.minimum(at // 128, (model - block) // 128) * 128
        gw = lax.dynamic_slice_in_dim(gw, at - first, size, axis=1)
    tile = (frames, rows, columns)
    return (
        attn.reshape(*tile, model),
        dq.reshape(*tile, width),
        dk.reshape(*tile, width),
        dv.reshape(*tile, width),
        gw,
    )


def solution(mesh):
    tile = P("tm", "height", None, None)
    return jax.shard_map(
        functools.partial(shards, mesh.shape["tm"], mesh.shape["height"]),
        mesh=mesh,
        in_specs=(tile, tile, tile, P("height", None), tile, P(), P()),
        out_specs=(tile, tile, tile, tile, P("height", "tm")),
        check_vma=False,
    )
```

```python
import functools
import math

import jax
import jax.numpy as jnp
import numpy as np
from jax import lax
from jax.experimental import pallas as pl
from jax.experimental.pallas import tpu as pltpu
from jax.sharding import PartitionSpec as P

HEAD_DIM = 128
HALO = 2
MESH = pl.DeviceIdType.MESH
F32 = jnp.float32
BF16 = jnp.bfloat16
SIDES = ((-1, 0), (1, 0), (0, -1), (0, 1), (-1, -1), (-1, 1), (1, -1), (1, 1))


def piece_sizes(frames, rows, columns):
    sizes = []
    for df, dr in SIDES:
        sizes.append((HALO if df else frames) * (HALO if dr else rows) * columns)
    return sizes


def key_table(frames, rows, columns):
    table = []
    for piece, (df, dr) in enumerate(((0, 0),) + SIDES):
        for f in range(HALO) if df else range(frames):
            for r in range(HALO) if dr else range(rows):
                fd = 0 if df == 0 else (HALO - f if df < 0 else f + 1)
                rd = 0 if dr == 0 else (HALO - r if dr < 0 else r + 1)
                table += [(piece, fd, rd)] * columns
    return np.ascontiguousarray(np.array(table, np.int32).T)


def piece_rows(df, dr, frames, rows, columns):
    fs = range(frames) if df == 0 else (range(frames - HALO, frames) if df < 0 else range(HALO))
    if dr == 0:
        return [(fs[0] * rows * columns, len(fs) * rows * columns)]
    first = (rows - HALO) if dr < 0 else 0
    return [((f * rows + first) * columns, HALO * columns) for f in fs]


def kernel(
    dims,
    q_ref, k_ref, v_ref, table_ref, reach_ref, valid_ref, w_hbm, og_hbm,
    attn_ref, dq_ref, dk_ref, dv_ref, gw_ref,
    wfull, ogown, ogcols, kvsend, kvext, gsend, grecv, prob, dmixed, mixed, mixall, acc, gpart, bias_ref, gwsend, gwrecv,
    local_sem, halo_s, halo_r, grad_s, grad_r, mix_s, mix_r,
    wr_s, wr_r, wl_s, wl_r, wc_s, wc_r, og_s, og_r, gw_s, gw_r,
):
    nt, nh, frames, rows, columns = dims
    t, h = lax.axis_index("tm"), lax.axis_index("height")
    tokens, width = q_ref.shape
    model = og_hbm.shape[1]
    share = w_hbm.shape[0]
    heads = width // HEAD_DIM
    half = model // 2
    window = gpart.shape[1]
    span_cols = model // nt
    scale = 1.0 / math.sqrt(HEAD_DIM)
    sizes = piece_sizes(frames, rows, columns)
    starts = [sum(sizes[:i]) for i in range(8)]

    def place(df, dr):
        return (lax.rem(t + nt + df, nt), lax.rem(h + nh + dr, nh))

    def exists(df, dr):
        a, b = t + df, h + dr
        return (a >= 0) & (a < nt) & (b >= 0) & (b < nh)

    def exchange(copies, sign, action):
        for (df, dr), copy in zip(SIDES, copies):
            if action == "start":
                pl.when(exists(sign * df, sign * dr))(copy.start)
            else:
                pl.when(exists(sign * df, sign * dr))(copy.wait_send)
                pl.when(exists(-sign * df, -sign * dr))(copy.wait_recv)

    def remote(src, dst, ssem, rsem, where):
        return pltpu.make_async_remote_copy(
            src_ref=src, dst_ref=dst, send_sem=ssem, recv_sem=rsem,
            device_id=where, device_id_type=MESH,
        )

    def wrow(j, lo=0, size=None):
        return pl.ds(pl.multiple_of(j * share + lo, 16), share if size is None else size)

    def orow(j, lo=0, size=None):
        return pl.ds(pl.multiple_of(j * tokens + lo, 16), tokens if size is None else size)

    own_w = pltpu.make_async_copy(w_hbm, wfull.at[wrow(h), :], local_sem.at[0])
    own_og = pltpu.make_async_copy(og_hbm, ogown, local_sem.at[1])
    own_w.start()
    own_og.start()

    barrier = pltpu.get_barrier_semaphore()
    greeted = 0
    for i in range(1, nh):
        pl.semaphore_signal(barrier, inc=1, device_id=(t, lax.rem(h + i, nh)), device_id_type=MESH)
        greeted += 1
    for i in range(1, nt):
        pl.semaphore_signal(barrier, inc=1, device_id=(lax.rem(t + i, nt), h), device_id_type=MESH)
        greeted += 1
    for df, dr in SIDES:
        if df and dr:
            pl.semaphore_signal(barrier, inc=1, device_id=place(df, dr), device_id_type=MESH)
            greeted += 1

    piece = table_ref[0:1, :]
    hit = jnp.ones_like(piece)
    for s, (df, dr) in enumerate(SIDES):
        a, b = place(df, dr)
        here = jnp.where(exists(df, dr), valid_ref[a, b], 0)
        hit = jnp.where(piece == s + 1, here, hit)
    near = (table_ref[1:2, :] <= reach_ref[t, h, 0]) & (table_ref[2:3, :] <= reach_ref[t, h, 1])
    bias_ref[...] = jnp.where((piece == 0) | (near & (hit == 1)), 0.0, -1e30)

    for i, ref in enumerate((k_ref, v_ref)):
        x = ref[...]
        kvext[i, 0:tokens, :] = x
        x = x.astype(F32)
        for s, (df, dr) in enumerate(SIDES):
            parts = [x[a : a + n] for a, n in piece_rows(df, dr, frames, rows, columns)]
            y = parts[0] if len(parts) == 1 else jnp.concatenate(parts, axis=0)
            kvsend[i, starts[s] : starts[s] + sizes[s], :] = y.astype(BF16)

    for s, (df, dr) in enumerate(SIDES):

        @pl.when(jnp.logical_not(exists(df, dr)))
        def _():
            rs = pl.ds(tokens + starts[s], sizes[s])
            kvext[:, rs, :] = jnp.zeros((2, sizes[s], width), BF16)

    par = lax.rem(h, 2)
    pos = (1 - par) * (h // 2) + par * (nh - 1 - h // 2)

    def at(p):
        p = lax.rem(p + nh, nh)
        far = p // (nh // 2)
        return (1 - far) * (2 * p) + far * (2 * (nh - 1 - p) + 1)

    right, left = (t, at(pos + 1)), (t, at(pos - 1))
    steps = nh // 2
    core = lax.rem(t, 2)
    partner = (t + 1 - 2 * core, h)
    mine = pl.ds(pl.multiple_of(core * half, 128), half)

    def span(step, size, side):
        if step < steps - 1:
            return 0, size
        return (0 if side == 0 else size // 2), size // 2

    def ring_sends(step, buf, rowfn, size, cols, sems):
        out = []
        for side, (target, sign) in enumerate(((right, -1), (left, 1))):
            lo, n = span(step, size, side)
            ref = buf.at[rowfn(at(pos + sign * step), lo, n), cols]
            ssem, rsem = sems[2 * side], sems[2 * side + 1]
            copy = remote(ref, ref, ssem.at[step], rsem.at[step], target)
            copy.start()
            out.append(copy)
        return out

    wsems = (wr_s, wr_r, wl_s, wl_r)
    def w_sends(step):
        return ring_sends(step, wfull, wrow, share, mine, wsems)

    def gw_sends(step):
        out = []
        for side, (target, sign) in enumerate(((right, 1), (left, -1))):
            base = at(pos + sign * (steps - step)) * share
            cut = share // 2
            for part in range(2):
                if step == 0 and part != side:
                    continue
                rs = slice(part * cut, (part + 1) * cut)
                total = gpart[pl.ds(pl.multiple_of(base + part * cut, 16), cut), :]
                if step > 1 or (step == 1 and part == side):
                    total += gwrecv[side, step - 1, rs, :].astype(F32)
                gwsend[side, step, rs, :] = total.astype(BF16)
            rs = pl.ds(side * cut, cut) if step == 0 else pl.ds(0, share)
            i = side * steps + step
            copy = remote(
                gwsend.at[side, step, rs, :], gwrecv.at[side, step, rs, :],
                gw_s.at[i], gw_r.at[i], target,
            )
            copy.start()
            out.append(copy)
        return out

    def cols_start(j):
        block = jnp.minimum((j * span_cols) // 128, (model - window) // 128)
        return pl.multiple_of(block * 128, 128)

    def share_sends(step):
        out = []
        for side, sign in enumerate((-1, 1)):
            lo, n = span(step, share, side)
            ref = wfull.at[wrow(at(pos + sign * (step + 1)), lo, n), mine]
            i = 2 * step + side
            out.append(remote(ref, ref, wc_s.at[i], wc_r.at[i], partner))
        for copy in out:
            copy.start()
        return out

    own_w.wait()
    own_og.wait()
    pl.semaphore_wait(barrier, greeted)
    halos = []
    for s, (df, dr) in enumerate(SIDES):
        copy = remote(
            kvsend.at[:, pl.ds(starts[s], sizes[s]), :],
            kvext.at[:, pl.ds(tokens + starts[s], sizes[s]), :],
            halo_s.at[s], halo_r.at[s], place(-df, -dr),
        )
        halos.append(copy)
    exchange(halos, -1, "start")
    live = w_sends(0)
    ogcols[orow(t), :] = ogown[:, pl.ds(cols_start(t), window)]
    gathers = []
    for i in range(1, nt):
        j = lax.rem(t + i, nt)
        copy = remote(
            ogown.at[:, pl.ds(cols_start(j), window)], ogcols.at[orow(t), :],
            og_s.at[i - 1], og_r.at[i - 1], (j, h),
        )
        copy.start()
        gathers.append(copy)
    shared = []

    def w_step(step):
        for copy in live:
            copy.wait()
        live.clear()
        if step < steps - 1:
            live.extend(w_sends(step + 1))
        shared.extend(share_sends(step))

    for step in range(2):
        w_step(step)
    exchange(halos, -1, "wait")

    group = 3 if heads % 3 == 0 else 1

    def cols_of(c):
        return pl.ds(pl.multiple_of(c * HEAD_DIM, HEAD_DIM), HEAD_DIM)

    def nt_dot(a, b):
        return lax.dot_general(a, b, (((1,), (1,)), ((), ())), preferred_element_type=F32)

    def tn_dot(a, b):
        return lax.dot_general(a, b, (((0,), (0,)), ((), ())), preferred_element_type=F32)

    def nn_dot(a, b):
        return lax.dot_general(a, b, (((1,), (0,)), ((), ())), preferred_element_type=F32)

    def forward(g, carry):
        for j in range(group):
            c = g * group + j
            cs = cols_of(c)
            scores = nt_dot(q_ref[:, cs], kvext[0, :, cs]) * scale + bias_ref[...]
            e = jnp.exp(scores - jnp.max(scores, axis=-1, keepdims=True))
            p = e / jnp.sum(e, axis=-1, keepdims=True)
            prob[c] = p
            mixed[:, cs] = nn_dot(p.astype(BF16), kvext[1, :, cs]).astype(BF16)
        return carry

    lax.fori_loop(0, heads // group, forward, 0)

    mixall[orow(t), :] = mixed[...]
    for i in range(1, nt):
        copy = remote(
            mixed, mixall.at[orow(t), :], mix_s.at[i - 1], mix_r.at[i - 1],
            (lax.rem(t + i, nt), h),
        )
        copy.start()
        gathers.append(copy)

    def gw_step(step):
        for copy in live:
            copy.wait()
        live.clear()
        if step < steps:
            live.extend(gw_sends(step))

    for step in range(2, steps):
        w_step(step)

    for copy in gathers:
        copy.wait()

    def weight(i, carry):
        cs = pl.ds(pl.multiple_of(i * 256, 256), 256)
        gpart[cs, :] = tn_dot(mixall[:, cs], ogcols[...])
        return carry

    lax.fori_loop(0, width // 256, weight, 0)
    gw_step(0)
    for copy in shared:
        copy.wait()

    def project(i, carry):
        r = pl.ds(pl.multiple_of(i * 256, 256), 256)
        dmixed[:, r] = nt_dot(ogown[...], wfull[r, :]).astype(BF16)
        return carry

    lax.fori_loop(0, width // 256, project, 0)

    gw_step(1)

    def backward(g, carry):
        for j in range(group):
            c = g * group + j
            cs = cols_of(c)
            p = prob[c]
            dm = dmixed[:, cs]
            dp = nt_dot(dm, kvext[1, :, cs])
            inner = jnp.sum(p * dp, axis=-1, keepdims=True)
            ds = (p * (dp - inner) * scale).astype(BF16)
            dq_ref[:, cs] = nn_dot(ds, kvext[0, :, cs]).astype(BF16)
            dk = tn_dot(ds, q_ref[:, cs])
            dv = tn_dot(p.astype(BF16), dm)
            acc[0, :, cs] = dk[:tokens]
            acc[1, :, cs] = dv[:tokens]
            gsend[0, :, cs] = dk[tokens:].astype(BF16)
            gsend[1, :, cs] = dv[tokens:].astype(BF16)
        return carry

    lax.fori_loop(0, heads // group, backward, 0)

    grads = []
    for s, (df, dr) in enumerate(SIDES):
        rs = pl.ds(starts[s], sizes[s])
        copy = remote(
            gsend.at[:, rs, :], grecv.at[:, rs, :], grad_s.at[s], grad_r.at[s], place(df, dr)
        )
        grads.append(copy)
    exchange(grads, 1, "start")
    gw_step(2)

    def attn(i, carry):
        cs = pl.ds(pl.multiple_of(i * 256, 256), 256)
        attn_ref[:, cs] = nn_dot(mixed[...], wfull[:, cs]).astype(BF16)
        return carry

    lax.fori_loop(0, model // 256, attn, 0)
    gw_step(3)

    exchange(grads, 1, "wait")
    for i, ref in enumerate((dk_ref, dv_ref)):
        for s, (df, dr) in enumerate(SIDES):

            @pl.when(exists(-df, -dr))
            def _():
                y = grecv[i, starts[s] : starts[s] + sizes[s], :].astype(F32)
                first = 0
                for a, n in piece_rows(df, dr, frames, rows, columns):
                    acc[i, a : a + n, :] += y[first : first + n]
                    first += n

        ref[...] = acc[i].astype(BF16)

    for step in range(4, steps + 1):
        gw_step(step)
    gw_ref[...] = (
        gpart[wrow(h), :]
        + gwrecv[0, steps - 1].astype(F32)
        + gwrecv[1, steps - 1].astype(F32)
    )


def shards(nt, nh, queries, key_tokens, value_tokens, out_weight, out_grad, window_reach, tile_valid):
    frames, rows, columns, width = queries.shape
    model = out_grad.shape[3]
    share = out_weight.shape[0]
    tokens = frames * rows * columns
    heads = width // HEAD_DIM
    halo = sum(piece_sizes(frames, rows, columns))
    ext = tokens + halo
    table = key_table(frames, rows, columns)
    narrow = (model // nt) % 128 == 0
    block = model // nt if narrow else 256
    steps = nh // 2
    vmem = pl.BlockSpec(memory_space=pltpu.VMEM)
    smem = pl.BlockSpec(memory_space=pltpu.SMEM)
    hbm = pl.BlockSpec(memory_space=pl.ANY)
    dma = pltpu.SemaphoreType.DMA
    attn, dq, dk, dv, gw = pl.pallas_call(
        functools.partial(kernel, (nt, nh, frames, rows, columns)),
        out_shape=(
            jax.ShapeDtypeStruct((tokens, model), BF16),
            jax.ShapeDtypeStruct((tokens, width), BF16),
            jax.ShapeDtypeStruct((tokens, width), BF16),
            jax.ShapeDtypeStruct((tokens, width), BF16),
            jax.ShapeDtypeStruct((share, block), F32),
        ),
        in_specs=[vmem, vmem, vmem, vmem, smem, smem, hbm, hbm],
        out_specs=[vmem] * 5,
        scratch_shapes=[
            pltpu.VMEM((width, model), BF16),
            pltpu.VMEM((tokens, model), BF16),
            pltpu.VMEM((nt * tokens, block), BF16),
            pltpu.VMEM((2, halo, width), BF16),
            pltpu.VMEM((2, ext, width), BF16),
            pltpu.VMEM((2, halo, width), BF16),
            pltpu.VMEM((2, halo, width), BF16),
            pltpu.VMEM((heads, tokens, ext), F32),
            pltpu.VMEM((tokens, width), BF16),
            pltpu.VMEM((tokens, width), BF16),
            pltpu.VMEM((nt * tokens, width), BF16),
            pltpu.VMEM((2, tokens, width), F32),
            pltpu.VMEM((width, block), F32),
            pltpu.VMEM((1, ext), F32),
            pltpu.VMEM((2, steps, share, block), BF16),
            pltpu.VMEM((2, steps, share, block), BF16),
            dma((2,)), dma((8,)), dma((8,)), dma((8,)), dma((8,)),
            dma((nt - 1,)), dma((nt - 1,)),
            dma((steps,)), dma((steps,)), dma((steps,)), dma((steps,)),
            dma((2 * steps,)), dma((2 * steps,)),
            dma((nt - 1,)), dma((nt - 1,)), dma((2 * steps,)), dma((2 * steps,)),
        ],
        compiler_params=pltpu.CompilerParams(
            collective_id=0, has_side_effects=True, vmem_limit_bytes=56 * 2**20
        ),
    )(
        queries.reshape(tokens, width),
        key_tokens.reshape(tokens, width),
        value_tokens.reshape(tokens, width),
        table,
        window_reach,
        tile_valid,
        out_weight,
        out_grad.reshape(tokens, model),
    )
    if not narrow:
        size = model // nt
        at = lax.axis_index("tm") * size
        first = jnp.minimum(at // 128, (model - block) // 128) * 128
        gw = lax.dynamic_slice_in_dim(gw, at - first, size, axis=1)
    tile = (frames, rows, columns)
    return (
        attn.reshape(*tile, model),
        dq.reshape(*tile, width),
        dk.reshape(*tile, width),
        dv.reshape(*tile, width),
        gw,
    )


def solution(mesh):
    tile = P("tm", "height", None, None)
    return jax.shard_map(
        functools.partial(shards, mesh.shape["tm"], mesh.shape["height"]),
        mesh=mesh,
        in_specs=(tile, tile, tile, P("height", None), tile, P(), P()),
        out_specs=(tile, tile, tile, tile, P("height", "tm")),
        check_vma=False,
    )
```
